512 devices in a mesh: mid: 128 (over x, y, z_hi, core), sub: 4 (over z_lo).
Axes of the slice: x: 4, y: 8, z: 8 (z_hi: 2, z_lo: 4; z = z_hi * 4 + z_lo), core: 2. Of those that a mesh axis runs over, the one named last changes fastest.
Arguments:
- signal: bfloat16 [393216, 1152], P(('mid', 'sub')), may hold values from -6 to 6
- col_basis: bfloat16 [393216, 256], P(('mid', 'sub')), may hold values from -0.21875 to 0.21875
- right_coupling: bfloat16 [512, 2, 256, 256], P(('mid', 'sub')), may hold values from -0.375 to 0.375
- middle_coupling: bfloat16 [512, 256, 256], P(('mid', 'sub')), may hold values from -0.375 to 0.375
- left_coupling: bfloat16 [512, 2, 256, 256], P(('mid', 'sub')), may hold values from -0.375 to 0.375
- row_basis: bfloat16 [393216, 256], P(('mid', 'sub')), may hold values from -0.375 to 0.375
- node_order: int32 [128], replicated, may hold values from 0 to 127, each once
Outputs:
- product: bfloat16 [393216, 1152], P(('mid', 'sub'))
The draws below stay inside these ranges and needn't reach their ends.
Inputs may be any that keep to these rules, and one draw needn't show every extreme that they name: node_order holds each of 0 to 127 exactly once.
All inputs are finite; a program needn't handle non-finite values.
Results may differ from the reference program's by a relative error of at most 0.013.
Values may be sent and summed in bfloat16 or wider, within the bound.
A program may use at most 64 MiB of HBM per device.

```python
import jax
import jax.numpy as jnp
from jax import lax

K = 256
LEAF = 768
R = 1152
NODES = 512
UNKNOWNS = 393216
N_MID = 128
N_SUB = 4


def shard_levels(own_key, extent, cuts, low, high):
    def one(dim, blocks):
        steps = jax.random.uniform(jax.random.fold_in(jax.random.fold_in(own_key, 6), dim), (blocks,), jnp.float32, low / len(cuts), high / len(cuts))
        return jnp.repeat(jnp.exp(steps), extent[dim] // blocks).reshape((-1,) + (1,) * (len(extent) - dim - 1))

    gain = one(*cuts[0])
    for cut in cuts[1:]:
        gain = gain * one(*cut)
    return gain


def centred(key, dims, spread, most, shards=(), kind=jnp.bfloat16):
    level = shard_levels(key, dims, shards, -0.22, 0.18) if shards else 1.0
    values = jax.random.normal(key, dims, jnp.float32) * spread * level
    return jnp.minimum(jnp.maximum(values, -most), most).astype(kind)


def setup_inputs(seed: int = 0) -> dict:
    key_list = jax.random.split(jax.random.key(seed), 8)
    return {
        "signal": centred(key_list[0], (UNKNOWNS, R), 1.0, 6.0, ((0, 512),)),
        "col_basis": centred(key_list[1], (UNKNOWNS, K), LEAF ** -0.5, 0.21875, ((0, 512),)),
        "right_coupling": centred(key_list[2], (NODES, 2, K, K), K ** -0.5, 0.375, ((0, 512),)),
        "middle_coupling": centred(key_list[3], (NODES, K, K), K ** -0.5, 0.375, ((0, 512),)),
        "left_coupling": centred(key_list[4], (NODES, 2, K, K), K ** -0.5, 0.375, ((0, 512),)),
        "row_basis": centred(key_list[5], (UNKNOWNS, K), K ** -0.5, 0.375, ((0, 512),)),
        "node_order": jax.random.permutation(key_list[6], N_MID).astype(jnp.int32),
    }


def apply_level(coeffs, coupling, bit):
    half = K // 2
    nodes = jnp.arange(N_SUB, dtype=jnp.int32)
    bitval = (nodes >> bit) & 1
    lower = nodes - bitval * (1 << bit)
    upper = lower + (1 << bit)
    top = coeffs[:, :half]
    bottom = coeffs[:, half:]
    chooser = (bitval == 1)[:, None, None]
    first = jnp.where(chooser, bottom[lower], top[lower])
    second = jnp.where(chooser, bottom[upper], top[upper])
    stacked = jnp.concatenate([first, second], axis=1)
    mixed = jnp.einsum("sij,sjr->sir", coupling.astype(jnp.float32), stacked.astype(jnp.float32))
    return mixed.astype(jnp.bfloat16)


def right_side(items):
    signal_blk, col_blk, right_blk = items
    coeffs = jnp.einsum("slk,slr->skr", col_blk.astype(jnp.float32), signal_blk.astype(jnp.float32)).astype(jnp.bfloat16)
    coeffs = apply_level(coeffs, right_blk[:, 0], 0)
    coeffs = apply_level(coeffs, right_blk[:, 1], 1)
    return coeffs


def left_side(items):
    gathered_blk, middle_blk, left_blk, row_blk = items
    coeffs = jnp.einsum("sij,sjr->sir", middle_blk.astype(jnp.float32), gathered_blk.astype(jnp.float32)).astype(jnp.bfloat16)
    coeffs = apply_level(coeffs, left_blk[:, 0], 1)
    coeffs = apply_level(coeffs, left_blk[:, 1], 0)
    result = jnp.einsum("slk,skr->slr", row_blk.astype(jnp.float32), coeffs.astype(jnp.float32))
    return result.astype(jnp.bfloat16)


def reference(signal, col_basis, right_coupling, middle_coupling, left_coupling, row_basis, node_order):
    pieces = K // N_MID
    signal_g = signal.reshape(N_MID, N_SUB, LEAF, R)
    col_g = col_basis.reshape(N_MID, N_SUB, LEAF, K)
    right_g = right_coupling.reshape(N_MID, N_SUB, 2, K, K)
    coeffs2 = lax.map(right_side, (signal_g, col_g, right_g))
    split = coeffs2.reshape(N_MID, N_SUB, N_MID, pieces, R)
    chosen = split[:, :, node_order.astype(jnp.int32)]
    gathered = jnp.transpose(chosen, (2, 1, 0, 3, 4)).reshape(N_MID, N_SUB, K, R)
    middle_g = middle_coupling.reshape(N_MID, N_SUB, K, K)
    left_g = left_coupling.reshape(N_MID, N_SUB, 2, K, K)
    row_g = row_basis.reshape(N_MID, N_SUB, LEAF, K)
    result = lax.map(left_side, (gathered, middle_g, left_g, row_g))
    return result.reshape(N_MID * N_SUB * LEAF, R)
```

```python
import jax
import jax.numpy as jnp
from jax import lax
from jax.experimental import pallas as pl
from jax.experimental.pallas import tpu as pltpu
from jax.sharding import PartitionSpec as P

MESH = pl.DeviceIdType.MESH
CHAIN = 55 << 20
EXPAND = 8 << 20
WIDTHS = (128,) * 9
LAG = (0, 3, 7, 11, 15, 18, 22, 25)
N = len(WIDTHS)
START = [sum(WIDTHS[:c]) for c in range(N)]
ORDER = [(s, c) for _, _, s, c in sorted((c + LAG[s], -s, s, c) for s in range(8) for c in range(N))]
RB0, RB1, ZH, YY, XC, LB1, LB0, SLOTS = 0, 1, 2, 3, 10, 17, 18, 19


def iota(shape, dim):
    return lax.broadcasted_iota(jnp.int32, shape, dim)


def onehot(hit):
    return jnp.where(hit, 1.0, 0.0).astype(jnp.bfloat16)


def mm(a, b):
    return jnp.dot(a, b, preferred_element_type=jnp.float32).astype(jnp.bfloat16)


def chain(
    sig_h, cb_h, rc_h, mc_h, lc_h, order, out, cb, rc, mc, lc, cbt, w0, w1, w2, w3, w4, p2,
    load, send, recv, *bufs,
):
    mid, sub = lax.axis_index("mid"), lax.axis_index("sub")
    core, zhi, y, x = mid % 2, (mid // 2) % 2, (mid // 4) % 8, mid // 32
    v0, v1 = sub % 2, sub // 2

    def cols(c):
        return slice(START[c], START[c] + WIDTHS[c])

    sig, own, outgo, come, near, ygot, xsend, xgot = (bufs[k * N : k * N + N] for k in range(8))

    def at(x_, y_, z_, c_):
        return ((x_ % 4 * 8 + y_ % 8) * 2 + z_ % 2) * 2 + c_ % 2, sub

    pair0 = (mid, sub + 1 - 2 * v0)
    pair1 = (mid, sub + 2 - 4 * v1)
    pairz = at(x, y, zhi + 1, core)
    ypeer = [at(x, y + k, zhi, core) for k in range(8)]
    xpeer = [at(x + j // 2, y, zhi, core + j % 2) for j in range(8)]
    ysrc = [at(x, y + 8 - k, zhi, core) for k in range(8)]
    xsrc = [at(x + 4 - j // 2, y, zhi, core + j % 2) for j in range(8)]

    barrier = pltpu.get_barrier_semaphore()
    greet = [pair0, pair1, pairz] + ysrc[1:] + xsrc[1:]
    for peer in greet:
        pl.semaphore_signal(barrier, inc=1, device_id=peer, device_id_type=MESH)

    loads = [pltpu.make_async_copy(cb_h, cb, load.at[0])]
    loads += [
        pltpu.make_async_copy(sig_h.at[:, cols(c)], sig[c], load.at[1 + c])
        for c in range(N)
    ]
    loads += [
        pltpu.make_async_copy(rc_h.at[0], rc, load.at[N + 1]),
        pltpu.make_async_copy(mc_h.at[0], mc, load.at[N + 2]),
        pltpu.make_async_copy(lc_h.at[0], lc, load.at[N + 3]),
    ]
    for copy in loads:
        copy.start()

    def half(v):
        return pl.ds(pl.multiple_of(v * 128, 128), 128)

    def swap(dst, src, rows, cols):
        for a, r in enumerate((rows, 1 - rows)):
            for b, q in enumerate((cols, 1 - cols)):
                dst[a * 128 : a * 128 + 128, b * 128 : b * 128 + 128] = src[half(r), half(q)]


    def copies(c):
        one = outgo[c]
        got = come[c]
        yield RB0, one.at[0], got.at[0], pair0
        yield RB1, one.at[1], got.at[1], pair1
        yield ZH, one.at[2], near[c].at[1], pairz
        for k in range(1, 8):
            yield YY + k - 1, near[c].at[:, pl.ds(k * 16, 16)], ygot[c].at[k], ypeer[k]
        for j in range(1, 8):
            yield XC + j - 1, xsend[c].at[j], xgot[c].at[j], xpeer[j]
        yield LB1, one.at[3], got.at[3], pair1
        yield LB0, one.at[4], got.at[4], pair0

    table = [
        {
            slot: pltpu.make_async_remote_copy(
                src_ref=src, dst_ref=dst, send_sem=send.at[c, slot], recv_sem=recv.at[c, slot],
                device_id=peer, device_id_type=MESH,
            )
            for slot, src, dst, peer in copies(c)
        }
        for c in range(N)
    ]

    def both(c, k):
        return jnp.concatenate([own[c][k], come[c][k]], axis=0)

    def split(c, k, value):
        outgo[c][k] = value[128:]
        own[c][k] = value[:128]

    def stage(s, c):
        hop = table[c]
        if s == 0:
            loads[1 + c].wait()
            split(c, 0, mm(cbt[...], sig[c][...]))
            hop[RB0].start()
        elif s == 1:
            hop[RB0].wait_recv()
            split(c, 1, mm(w0[...], both(c, 0)))
            hop[RB1].start()
        elif s == 2:
            hop[RB1].wait_recv()
            value = mm(w1[...], both(c, 1))
            outgo[c][2] = value[128:]
            near[c][0] = value[:128]
            hop[ZH].start()
        elif s == 3:
            hop[ZH].wait_recv()
            for k in (4, 3, 5, 2, 6, 1, 7):
                hop[YY + k - 1].start()
        elif s == 4:
            for k in range(1, 8):
                hop[YY + k - 1].wait_recv()
            value = jnp.concatenate(
                [near[c][0, 0:16], near[c][1, 0:16]] + [ygot[c][k].reshape(32, WIDTHS[c]) for k in range(1, 8)],
                axis=0,
            )
            xsend[c][...] = mm(p2[...], value).reshape(8, 32, WIDTHS[c])
            for j in (4, 5, 2, 3, 6, 7, 1):
                hop[XC + j - 1].start()
        elif s == 5:
            for j in range(1, 8):
                hop[XC + j - 1].wait_recv()
            value = jnp.concatenate([xsend[c][0]] + [xgot[c][j] for j in range(1, 8)], axis=0)
            split(c, 3, mm(w2[...], value))
            hop[LB1].start()
        elif s == 6:
            hop[LB1].wait_recv()
            split(c, 4, mm(w3[...], both(c, 3)))
            hop[LB0].start()
        else:
            hop[LB0].wait_recv()
            out[:, cols(c)] = mm(w4[...], both(c, 4))

    loads[0].wait()
    cbt[0:128] = cb[:, half(v0)].T
    cbt[128:256] = cb[:, half(1 - v0)].T

    def prepare():
        r = iota((256, 128), 0)
        dest = (
            ((((r >> 2) & 3) + x & 3) * 8 + (((r >> 4) & 7) + y & 7)) * 4
            + ((r >> 7) + zhi & 1) * 2
            + (((r >> 1) & 1) + core & 1)
        )
        piece = jnp.sum(
            jnp.where(iota((256, 128), 1) == dest, order[...].astype(jnp.float32), 0.0),
            axis=1, keepdims=True,
        ).astype(jnp.int32)
        row, col = iota((256, 256), 0), iota((256, 256), 1)
        pick = onehot(col == piece * 2 + (row & 1))
        p2[...] = onehot(
            col == ((row >> 2) & 7) * 32 + ((row >> 1) & 1) * 16 + (row >> 5) * 2 + (row & 1)
        )
        sx, sc, sy, sz = col >> 6, (col >> 5) & 1, (col >> 2) & 7, (col >> 1) & 1
        source = (
            ((x + 4 - sx & 3) * 8 + (y + 8 - sy & 7)) * 4 + (zhi + sz & 1) * 2 + (core + sc & 1)
        ) * 2 + (col & 1)
        place = onehot(row == source)
        for copy in loads[N + 1 :]:
            copy.wait()
        swap(w0, rc.at[0], v1, v0)
        for b, q in enumerate((v1, 1 - v1)):
            w3[:, b * 128 : b * 128 + 128] = rc[1, :, half(q)]
        w1[...] = mm(pick, w3[...])
        w4[...] = mm(mc[...], place)
        w2[0:128] = w4[half(v1), :]
        w2[128:256] = w4[half(1 - v1), :]
        swap(w3, lc.at[0], v0, v1)
        for b, q in enumerate((v0, 1 - v0)):
            w4[:, b * 128 : b * 128 + 128] = lc[1, :, half(q)]

    first = True
    for s, c in ORDER:
        if s == 0 and c == 0:
            loads[1].wait()
            split(0, 0, mm(cbt[...], sig[0][...]))
            pl.semaphore_wait(barrier, len(greet))
            table[0][RB0].start()
            continue
        if s == 1 and first:
            prepare()
            first = False
        stage(s, c)
    for hop in table:
        for copy in hop.values():
            copy.wait_send()


def expand(rb, c5, out, tile, sem):
    rows = tile.shape[1]
    copies = []
    for i in range(tile.shape[0]):
        block = slice(i * rows, i * rows + rows)
        tile[i] = mm(rb[block], c5[...])
        copies.append(pltpu.make_async_copy(tile.at[i], out.at[block], sem.at[i]))
        copies[-1].start()
    for copy in copies:
        copy.wait()


def local(signal, col_basis, right_coupling, middle_coupling, left_coupling, row_basis, node_order):
    bf = jnp.bfloat16
    V = pltpu.VMEM
    hbm = pl.BlockSpec(memory_space=pl.ANY)
    vmem = pl.BlockSpec(memory_space=V)
    coeffs = pl.pallas_call(
        chain,
        name="chain",
        out_shape=V((256, signal.shape[1]), bf),
        in_specs=[hbm] * 5 + [vmem],
        out_specs=vmem,
        scratch_shapes=[
            V((768, 256), bf), V((2, 256, 256), bf), V((256, 256), bf), V((2, 256, 256), bf), V((256, 768), bf),
        ]
        + [V((256, 256), bf)] * 6
        + [
            pltpu.SemaphoreType.DMA((N + 4,)),
            pltpu.SemaphoreType.DMA((N, SLOTS)),
            pltpu.SemaphoreType.DMA((N, SLOTS)),
        ]
        + [
            V((*shape, width), bf)
            for shape in (
                (768,), (5, 128), (5, 128), (5, 128), (2, 128), (8, 2, 16), (8, 32), (8, 32)
            )
            for width in WIDTHS
        ],
        compiler_params=pltpu.CompilerParams(collective_id=0, has_side_effects=True, vmem_limit_bytes=CHAIN),
    )(signal, col_basis, right_coupling, middle_coupling, left_coupling, node_order.reshape(1, 128))
    rows, block = row_basis.shape[0], 128
    return pl.pallas_call(
        expand,
        name="expand",
        out_shape=jax.ShapeDtypeStruct((rows, signal.shape[1]), bf),
        in_specs=[vmem, vmem],
        out_specs=hbm,
        scratch_shapes=[
            V((rows // block, block, signal.shape[1]), bf), pltpu.SemaphoreType.DMA((rows // block,))
        ],
        compiler_params=pltpu.CompilerParams(vmem_limit_bytes=EXPAND),
    )(row_basis, coeffs)


def solution(mesh):
    return jax.shard_map(
        local,
        mesh=mesh,
        in_specs=(
            P(("mid", "sub"), None),
            P(("mid", "sub"), None),
            P(("mid", "sub"), None, None, None),
            P(("mid", "sub"), None, None),
            P(("mid", "sub"), None, None, None),
            P(("mid", "sub"), None),
            P(),
        ),
        out_specs=P(("mid", "sub"), None),
        check_vma=False,
    )
```

```python
import jax
import jax.numpy as jnp
from jax import lax
from jax.experimental import pallas as pl
from jax.experimental.pallas import tpu as pltpu
from jax.sharding import PartitionSpec as P

MESH = pl.DeviceIdType.MESH
CHAIN = 55 << 20
EXPAND = 8 << 20
WIDTHS = (128,) * 9
LAG = (0, 4, 8, 12, 16, 20, 24, 28)
N = len(WIDTHS)
START = [sum(WIDTHS[:c]) for c in range(N)]
ORDER = [(s, c) for _, _, s, c in sorted((c + LAG[s], -s, s, c) for s in range(8) for c in range(N))]
RB0, RB1, ZH, YY, XC, LB1, LB0, SLOTS = 0, 1, 2, 3, 4, 5, 6, 7


def iota(shape, dim):
    return lax.broadcasted_iota(jnp.int32, shape, dim)


def onehot(hit):
    return jnp.where(hit, 1.0, 0.0).astype(jnp.bfloat16)


def mm(a, b):
    return jnp.dot(a, b, preferred_element_type=jnp.float32).astype(jnp.bfloat16)


def chain(
    sig_h, cb_h, rc_h, mc_h, lc_h, order, out, cb, rc, mc, lc, cbt, w0, w1, w2, w3, w4, p2,
    sent, load, send, recv, *bufs,
):
    mid, sub = lax.axis_index("mid"), lax.axis_index("sub")
    core, zhi, y, x = mid % 2, (mid // 2) % 2, (mid // 4) % 8, mid // 32
    v0, v1 = sub % 2, sub // 2

    def cols(c):
        return slice(START[c], START[c] + WIDTHS[c])

    sig, own, outgo, come, near, ygot, xsend, xgot = (bufs[k * N : k * N + N] for k in range(8))

    def at(x_, y_, z_, c_):
        return ((x_ % 4 * 8 + y_ % 8) * 2 + z_ % 2) * 2 + c_ % 2, sub

    pair0 = (mid, sub + 1 - 2 * v0)
    pair1 = (mid, sub + 2 - 4 * v1)
    pairz = at(x, y, zhi + 1, core)
    ypeer = [at(x, y + k, zhi, core) for k in range(8)]
    xpeer = [at(x + j // 2, y, zhi, core + j % 2) for j in range(8)]
    ysrc = [at(x, y + 8 - k, zhi, core) for k in range(8)]
    xsrc = [at(x + 4 - j // 2, y, zhi, core + j % 2) for j in range(8)]

    barrier = pltpu.get_barrier_semaphore()
    greet = [pair0, pair1, pairz] + ysrc[1:] + xsrc[1:]
    for peer in greet:
        pl.semaphore_signal(barrier, inc=1, device_id=peer, device_id_type=MESH)

    loads = [pltpu.make_async_copy(cb_h, cb, load.at[0])]
    loads += [
        pltpu.make_async_copy(sig_h.at[:, cols(c)], sig[c], load.at[1 + c])
        for c in range(N)
    ]
    loads += [
        pltpu.make_async_copy(rc_h.at[0], rc, load.at[N + 1]),
        pltpu.make_async_copy(mc_h.at[0], mc, load.at[N + 2]),
        pltpu.make_async_copy(lc_h.at[0], lc, load.at[N + 3]),
    ]
    for copy in loads:
        copy.start()

    def half(v):
        return pl.ds(pl.multiple_of(v * 128, 128), 128)

    def swap(dst, src, rows, cols):
        for a, r in enumerate((rows, 1 - rows)):
            for b, q in enumerate((cols, 1 - cols)):
                dst[a * 128 : a * 128 + 128, b * 128 : b * 128 + 128] = src[half(r), half(q)]


    def remote(c, slot, src, dst, peer):
        pltpu.make_async_remote_copy(
            src_ref=src, dst_ref=dst, send_sem=send.at[0], recv_sem=recv.at[c, slot],
            device_id=peer, device_id_type=MESH,
        ).start()

    def arrived(c, slot, dst):
        pltpu.make_async_copy(dst, dst, recv.at[c, slot]).wait()

    def both(c, k):
        return jnp.concatenate([own[c][k], come[c][k]], axis=0)

    def split(c, k, value):
        outgo[c][k] = value[128:]
        own[c][k] = value[:128]

    def stage(s, c):
        if s == 0:
            loads[1 + c].wait()
            split(c, 0, mm(cbt[...], sig[c][...]))
            remote(c, RB0, outgo[c].at[0], come[c].at[0], pair0)
        elif s == 1:
            arrived(c, RB0, come[c].at[0])
            split(c, 1, mm(w0[...], both(c, 0)))
            remote(c, RB1, outgo[c].at[1], come[c].at[1], pair1)
        elif s == 2:
            arrived(c, RB1, come[c].at[1])
            value = mm(w1[...], both(c, 1))
            outgo[c][2] = value[128:]
            near[c][0] = value[:128]
            remote(c, ZH, outgo[c].at[2], near[c].at[1], pairz)
        elif s == 3:
            arrived(c, ZH, near[c].at[1])
            for k in (4, 3, 5, 2, 6, 1, 7):
                remote(c, YY, near[c].at[:, pl.ds(k * 16, 16)], ygot[c].at[k], ypeer[k])
        elif s == 4:
            arrived(c, YY, ygot[c].at[1:8])
            value = jnp.concatenate(
                [near[c][0, 0:16], near[c][1, 0:16]] + [ygot[c][k].reshape(32, WIDTHS[c]) for k in range(1, 8)],
                axis=0,
            )
            xsend[c][...] = mm(p2[...], value).reshape(8, 32, WIDTHS[c])
            for j in (4, 5, 2, 3, 6, 7, 1):
                remote(c, XC, xsend[c].at[j], xgot[c].at[j], xpeer[j])
        elif s == 5:
            arrived(c, XC, xgot[c].at[1:8])
            value = jnp.concatenate([xsend[c][0]] + [xgot[c][j] for j in range(1, 8)], axis=0)
            split(c, 3, mm(w2[...], value))
            remote(c, LB1, outgo[c].at[3], come[c].at[3], pair1)
        elif s == 6:
            arrived(c, LB1, come[c].at[3])
            split(c, 4, mm(w3[...], both(c, 3)))
            remote(c, LB0, outgo[c].at[4], come[c].at[4], pair0)
        else:
            arrived(c, LB0, come[c].at[4])
            out[:, cols(c)] = mm(w4[...], both(c, 4))

    loads[0].wait()
    cbt[0:128] = cb[:, half(v0)].T
    cbt[128:256] = cb[:, half(1 - v0)].T

    def prepare():
        r = iota((256, 128), 0)
        dest = (
            ((((r >> 2) & 3) + x & 3) * 8 + (((r >> 4) & 7) + y & 7)) * 4
            + ((r >> 7) + zhi & 1) * 2
            + (((r >> 1) & 1) + core & 1)
        )
        piece = jnp.sum(
            jnp.where(iota((256, 128), 1) == dest, order[...].astype(jnp.float32), 0.0),
            axis=1, keepdims=True,
        ).astype(jnp.int32)
        row, col = iota((256, 256), 0), iota((256, 256), 1)
        pick = onehot(col == piece * 2 + (row & 1))
        p2[...] = onehot(
            col == ((row >> 2) & 7) * 32 + ((row >> 1) & 1) * 16 + (row >> 5) * 2 + (row & 1)
        )
        sx, sc, sy, sz = col >> 6, (col >> 5) & 1, (col >> 2) & 7, (col >> 1) & 1
        source = (
            ((x + 4 - sx & 3) * 8 + (y + 8 - sy & 7)) * 4 + (zhi + sz & 1) * 2 + (core + sc & 1)
        ) * 2 + (col & 1)
        place = onehot(row == source)
        for copy in loads[N + 1 :]:
            copy.wait()
        swap(w0, rc.at[0], v1, v0)
        for b, q in enumerate((v1, 1 - v1)):
            w3[:, b * 128 : b * 128 + 128] = rc[1, :, half(q)]
        w1[...] = mm(pick, w3[...])
        w4[...] = mm(mc[...], place)
        w2[0:128] = w4[half(v1), :]
        w2[128:256] = w4[half(1 - v1), :]
        swap(w3, lc.at[0], v0, v1)
        for b, q in enumerate((v0, 1 - v0)):
            w4[:, b * 128 : b * 128 + 128] = lc[1, :, half(q)]

    first = True
    for s, c in ORDER:
        if s == 0 and c == 0:
            loads[1].wait()
            split(0, 0, mm(cbt[...], sig[0][...]))
            pl.semaphore_wait(barrier, len(greet))
            remote(0, RB0, outgo[0].at[0], come[0].at[0], pair0)
            continue
        if s == 1 and first:
            prepare()
            first = False
        stage(s, c)
    pltpu.make_async_copy(sent, sent, send.at[0]).wait()


def expand(rb, c5, out, tile, sem):
    rows = tile.shape[1]
    copies = []
    for i in range(tile.shape[0]):
        block = slice(i * rows, i * rows + rows)
        tile[i] = mm(rb[block], c5[...])
        copies.append(pltpu.make_async_copy(tile.at[i], out.at[block], sem.at[i]))
        copies[-1].start()
    for copy in copies:
        copy.wait()


def local(signal, col_basis, right_coupling, middle_coupling, left_coupling, row_basis, node_order):
    bf = jnp.bfloat16
    V = pltpu.VMEM
    hbm = pl.BlockSpec(memory_space=pl.ANY)
    vmem = pl.BlockSpec(memory_space=V)
    coeffs = pl.pallas_call(
        chain,
        name="chain",
        out_shape=V((256, signal.shape[1]), bf),
        in_specs=[hbm] * 5 + [vmem],
        out_specs=vmem,
        scratch_shapes=[
            V((768, 256), bf), V((2, 256, 256), bf), V((256, 256), bf), V((2, 256, 256), bf), V((256, 768), bf),
        ]
        + [V((256, 256), bf)] * 6
        + [
            V((1088, signal.shape[1]), bf),
            pltpu.SemaphoreType.DMA((N + 4,)),
            pltpu.SemaphoreType.DMA((1,)),
            pltpu.SemaphoreType.DMA((N, SLOTS)),
        ]
        + [
            V((*shape, width), bf)
            for shape in (
                (768,), (5, 128), (5, 128), (5, 128), (2, 128), (8, 2, 16), (8, 32), (8, 32)
            )
            for width in WIDTHS
        ],
        compiler_params=pltpu.CompilerParams(collective_id=0, has_side_effects=True, vmem_limit_bytes=CHAIN),
    )(signal, col_basis, right_coupling, middle_coupling, left_coupling, node_order.reshape(1, 128))
    rows, block = row_basis.shape[0], 128
    return pl.pallas_call(
        expand,
        name="expand",
        out_shape=jax.ShapeDtypeStruct((rows, signal.shape[1]), bf),
        in_specs=[vmem, vmem],
        out_specs=hbm,
        scratch_shapes=[
            V((rows // block, block, signal.shape[1]), bf), pltpu.SemaphoreType.DMA((rows // block,))
        ],
        compiler_params=pltpu.CompilerParams(vmem_limit_bytes=EXPAND),
    )(row_basis, coeffs)


def solution(mesh):
    return jax.shard_map(
        local,
        mesh=mesh,
        in_specs=(
            P(("mid", "sub"), None),
            P(("mid", "sub"), None),
            P(("mid", "sub"), None, None, None),
            P(("mid", "sub"), None, None),
            P(("mid", "sub"), None, None, None),
            P(("mid", "sub"), None),
            P(),
        ),
        out_specs=P(("mid", "sub"), None),
        check_vma=False,
    )
```

```python
import jax
import jax.numpy as jnp
from jax import lax
from jax.experimental import pallas as pl
from jax.experimental.pallas import tpu as pltpu
from jax.sharding import PartitionSpec as P

MESH = pl.DeviceIdType.MESH
CHAIN = 55 << 20
EXPAND = 8 << 20
WIDTHS = (128,) * 9
LAG = (0, 2, 5, 8, 12, 14, 17, 21)
N = len(WIDTHS)
START = [sum(WIDTHS[:c]) for c in range(N)]
ORDER = [(s, c) for _, _, s, c in sorted((c + LAG[s], -s, s, c) for s in range(8) for c in range(N))]
RB0, RB1, ZH, YY, XC, LB1, LB0, SLOTS = 0, 1, 2, 3, 4, 5, 6, 7


def iota(shape, dim):
    return lax.broadcasted_iota(jnp.int32, shape, dim)


def onehot(hit):
    return jnp.where(hit, 1.0, 0.0).astype(jnp.bfloat16)


def mm(a, b):
    return jnp.dot(a, b, preferred_element_type=jnp.float32).astype(jnp.bfloat16)


def chain(
    sig_h, cb_h, rc_h, mc_h, lc_h, order_h, out, order, sig, cb, mats, cbt, w0, w1, w2, w3, w4, p2,
    sent, load, send, recv, *bufs,
):
    mid, sub = lax.axis_index("mid"), lax.axis_index("sub")
    core, zhi, y, x = mid % 2, (mid // 2) % 2, (mid // 4) % 8, mid // 32
    v0, v1 = sub % 2, sub // 2

    def cols(c):
        return slice(START[c], START[c] + WIDTHS[c])

    own, outgo, come, near, ygot, xsend, xgot = (bufs[k * N : k * N + N] for k in range(7))
    rc, mc, lc = mats.at[0:2], mats.at[2], mats.at[3:5]

    loads = [pltpu.make_async_copy(cb_h, cb, load.at[0])]
    loads += [
        pltpu.make_async_copy(sig_h.at[:, cols(c)], sig.at[c], load.at[min(c, 1) + 1]) for c in range(N)
    ]
    loads += [
        pltpu.make_async_copy(rc_h.at[0], rc, load.at[3]),
        pltpu.make_async_copy(mc_h.at[0], mc, load.at[3]),
        pltpu.make_async_copy(lc_h.at[0], lc, load.at[3]),
        pltpu.make_async_copy(order_h, order, load.at[4]),
    ]
    for copy in loads[:2]:
        copy.start()

    def at(x_, y_, z_, c_):
        return ((x_ % 4 * 8 + y_ % 8) * 2 + z_ % 2) * 2 + c_ % 2, sub

    pair0 = (mid, sub + 1 - 2 * v0)
    pair1 = (mid, sub + 2 - 4 * v1)
    pairz = at(x, y, zhi + 1, core)
    ypeer = [at(x, y + k, zhi, core) for k in range(8)]
    xpeer = [at(x + j // 2, y, zhi, core + j % 2) for j in range(8)]
    ysrc = [at(x, y + 8 - k, zhi, core) for k in range(8)]
    xsrc = [at(x + 4 - j // 2, y, zhi, core + j % 2) for j in range(8)]

    barrier = pltpu.get_barrier_semaphore()
    greet = [pair0, pair1, pairz] + ysrc[1:] + xsrc[1:]
    for peer in greet:
        pl.semaphore_signal(barrier, inc=1, device_id=peer, device_id_type=MESH)

    def half(v):
        return pl.ds(pl.multiple_of(v * 128, 128), 128)

    def swap(dst, src, rows, cols):
        for a, r in enumerate((rows, 1 - rows)):
            for b, q in enumerate((cols, 1 - cols)):
                dst[a * 128 : a * 128 + 128, b * 128 : b * 128 + 128] = src[half(r), half(q)]


    def remote(c, slot, src, dst, peer):
        pltpu.make_async_remote_copy(
            src_ref=src, dst_ref=dst, send_sem=send.at[0], recv_sem=recv.at[c, slot],
            device_id=peer, device_id_type=MESH,
        ).start()

    def arrived(c, slot, dst):
        pltpu.make_async_copy(dst, dst, recv.at[c, slot]).wait()

    def both(c, k):
        return jnp.concatenate([own[c][k], come[c][k]], axis=0)

    def split(c, k, value):
        outgo[c][k] = value[128:]
        own[c][k] = value[:128]

    def stage(s, c):
        if s == 0:
            if c == 1:
                pltpu.make_async_copy(sig.at[1:N], sig.at[1:N], load.at[2]).wait()
            split(c, 0, mm(cbt[...], sig[c]))
            remote(c, RB0, outgo[c].at[0], come[c].at[0], pair0)
        elif s == 1:
            arrived(c, RB0, come[c].at[0])
            split(c, 1, mm(w0[...], both(c, 0)))
            remote(c, RB1, outgo[c].at[1], come[c].at[1], pair1)
        elif s == 2:
            arrived(c, RB1, come[c].at[1])
            value = mm(w1[...], both(c, 1))
            outgo[c][2] = value[128:]
            near[c][0] = value[:128]
            remote(c, ZH, outgo[c].at[2], near[c].at[1], pairz)
        elif s == 3:
            arrived(c, ZH, near[c].at[1])
            for k in (4, 3, 5, 2, 6, 1, 7):
                remote(c, YY, near[c].at[:, pl.ds(k * 16, 16)], ygot[c].at[k], ypeer[k])
        elif s == 4:
            arrived(c, YY, ygot[c].at[1:8])
            value = jnp.concatenate(
                [near[c][0, 0:16], near[c][1, 0:16]] + [ygot[c][k].reshape(32, WIDTHS[c]) for k in range(1, 8)],
                axis=0,
            )
            xsend[c][...] = mm(p2[...], value).reshape(8, 32, WIDTHS[c])
            for j in (4, 5, 2, 3, 6, 7, 1):
                remote(c, XC, xsend[c].at[j], xgot[c].at[j], xpeer[j])
        elif s == 5:
            arrived(c, XC, xgot[c].at[1:8])
            value = jnp.concatenate([xsend[c][0]] + [xgot[c][j] for j in range(1, 8)], axis=0)
            split(c, 3, mm(w2[...], value))
            remote(c, LB1, outgo[c].at[3], come[c].at[3], pair1)
        elif s == 6:
            arrived(c, LB1, come[c].at[3])
            split(c, 4, mm(w3[...], both(c, 3)))
            remote(c, LB0, outgo[c].at[4], come[c].at[4], pair0)
        else:
            arrived(c, LB0, come[c].at[4])
            out[:, cols(c)] = mm(w4[...], both(c, 4))

    loads[0].wait()
    for copy in loads[2:]:
        copy.start()
    cbt[0:128] = cb[:, half(v0)].T
    cbt[128:256] = cb[:, half(1 - v0)].T

    def prepare():
        loads[-1].wait()
        r = iota((256, 128), 0)
        dest = (
            ((((r >> 2) & 3) + x & 3) * 8 + (((r >> 4) & 7) + y & 7)) * 4
            + ((r >> 7) + zhi & 1) * 2
            + (((r >> 1) & 1) + core & 1)
        )
        piece = jnp.sum(
            jnp.where(iota((256, 128), 1) == dest, order[...].astype(jnp.float32), 0.0),
            axis=1, keepdims=True,
        ).astype(jnp.int32)
        row, col = iota((256, 256), 0), iota((256, 256), 1)
        pick = onehot(col == piece * 2 + (row & 1))
        p2[...] = onehot(
            col == ((row >> 2) & 7) * 32 + ((row >> 1) & 1) * 16 + (row >> 5) * 2 + (row & 1)
        )
        sx, sc, sy, sz = col >> 6, (col >> 5) & 1, (col >> 2) & 7, (col >> 1) & 1
        source = (
            ((x + 4 - sx & 3) * 8 + (y + 8 - sy & 7)) * 4 + (zhi + sz & 1) * 2 + (core + sc & 1)
        ) * 2 + (col & 1)
        place = onehot(row == source)
        pltpu.make_async_copy(mats, mats, load.at[3]).wait()
        swap(w0, rc.at[0], v1, v0)
        for b, q in enumerate((v1, 1 - v1)):
            w3[:, b * 128 : b * 128 + 128] = rc[1, :, half(q)]
        w1[...] = mm(pick, w3[...])
        w4[...] = mm(mc[...], place)
        w2[0:128] = w4[half(v1), :]
        w2[128:256] = w4[half(1 - v1), :]
        swap(w3, lc.at[0], v0, v1)
        for b, q in enumerate((v0, 1 - v0)):
            w4[:, b * 128 : b * 128 + 128] = lc[1, :, half(q)]

    first = True
    for s, c in ORDER:
        if s == 0 and c == 0:
            loads[1].wait()
            split(0, 0, mm(cbt[...], sig[0]))
            pl.semaphore_wait(barrier, len(greet))
            remote(0, RB0, outgo[0].at[0], come[0].at[0], pair0)
            continue
        if s == 1 and first:
            prepare()
            first = False
        stage(s, c)
    pltpu.make_async_copy(sent, sent, send.at[0]).wait()


def expand(rb, c5, out, tile, sem):
    rows = tile.shape[1]
    copies = []
    for i in range(tile.shape[0]):
        block = slice(i * rows, i * rows + rows)
        tile[i] = mm(rb[block], c5[...])
        copies.append(pltpu.make_async_copy(tile.at[i], out.at[block], sem.at[i]))
        copies[-1].start()
    for copy in copies:
        copy.wait()


def local(signal, col_basis, right_coupling, middle_coupling, left_coupling, row_basis, node_order):
    bf = jnp.bfloat16
    V = pltpu.VMEM
    hbm = pl.BlockSpec(memory_space=pl.ANY)
    vmem = pl.BlockSpec(memory_space=V)
    coeffs = pl.pallas_call(
        chain,
        name="chain",
        out_shape=V((256, signal.shape[1]), bf),
        in_specs=[hbm] * 6,
        out_specs=vmem,
        scratch_shapes=[
            V((1, 128), jnp.int32), V((N, 768, WIDTHS[0]), bf), V((768, 256), bf), V((5, 256, 256), bf), V((256, 768), bf),
        ]
        + [V((256, 256), bf)] * 6
        + [
            V((1088, signal.shape[1]), bf),
            pltpu.SemaphoreType.DMA((5,)),
            pltpu.SemaphoreType.DMA((1,)),
            pltpu.SemaphoreType.DMA((N, SLOTS)),
        ]
        + [
            V((*shape, width), bf)
            for shape in (
                (5, 128), (5, 128), (5, 128), (2, 128), (8, 2, 16), (8, 32), (8, 32)
            )
            for width in WIDTHS
        ],
        compiler_params=pltpu.CompilerParams(collective_id=0, has_side_effects=True, vmem_limit_bytes=CHAIN),
    )(signal, col_basis, right_coupling, middle_coupling, left_coupling, node_order.reshape(1, 128))
    rows, block = row_basis.shape[0], 128
    return pl.pallas_call(
        expand,
        name="expand",
        out_shape=jax.ShapeDtypeStruct((rows, signal.shape[1]), bf),
        in_specs=[vmem, vmem],
        out_specs=hbm,
        scratch_shapes=[
            V((rows // block, block, signal.shape[1]), bf), pltpu.SemaphoreType.DMA((rows // block,))
        ],
        compiler_params=pltpu.CompilerParams(vmem_limit_bytes=EXPAND),
    )(row_basis, coeffs)


def solution(mesh):
    return jax.shard_map(
        local,
        mesh=mesh,
        in_specs=(
            P(("mid", "sub"), None),
            P(("mid", "sub"), None),
            P(("mid", "sub"), None, None, None),
            P(("mid", "sub"), None, None),
            P(("mid", "sub"), None, None, None),
            P(("mid", "sub"), None),
            P(),
        ),
        out_specs=P(("mid", "sub"), None),
        check_vma=False,
    )
```

```python
import jax
import jax.numpy as jnp
from jax import lax
from jax.experimental import pallas as pl
from jax.experimental.pallas import tpu as pltpu
from jax.sharding import PartitionSpec as P

MESH = pl.DeviceIdType.MESH
CHAIN = 55 << 20
EXPAND = 8 << 20
WIDTHS = (128,) * 9
LAG = (0, 2, 5, 8, 11, 14, 17, 21)
N = len(WIDTHS)
START = [sum(WIDTHS[:c]) for c in range(N)]
ORDER = [(s, c) for _, _, s, c in sorted((c + LAG[s], -s, s, c) for s in range(8) for c in range(N))]
RB0, RB1, ZH, YY, XC, LB1, LB0, SLOTS = 0, 1, 2, 3, 4, 5, 6, 7


def iota(shape, dim):
    return lax.broadcasted_iota(jnp.int32, shape, dim)


def onehot(hit):
    return jnp.where(hit, 1.0, 0.0).astype(jnp.bfloat16)


def mm(a, b):
    return jnp.dot(a, b, preferred_element_type=jnp.float32).astype(jnp.bfloat16)


def chain(
    sig_h, cb_h, rc_h, mc_h, lc_h, order_h, out, order, sig, cb, mats, cbt, w0, w1, w2, w3, w4, p2,
    sent, load, send, recv, *bufs,
):
    mid, sub = lax.axis_index("mid"), lax.axis_index("sub")
    core, zhi, y, x = mid % 2, (mid // 2) % 2, (mid // 4) % 8, mid // 32
    v0, v1 = sub % 2, sub // 2

    def cols(c):
        return slice(START[c], START[c] + WIDTHS[c])

    own, outgo, come, near, ygot, xsend, xgot = (bufs[k * N : k * N + N] for k in range(7))
    rc, mc, lc = mats.at[0:2], mats.at[2], mats.at[3:5]

    loads = [pltpu.make_async_copy(cb_h, cb, load.at[0])]
    loads += [
        pltpu.make_async_copy(sig_h.at[:, cols(c)], sig.at[c], load.at[min(c, 1) + 1]) for c in range(N)
    ]
    loads += [
        pltpu.make_async_copy(rc_h.at[0], rc, load.at[3]),
        pltpu.make_async_copy(mc_h.at[0], mc, load.at[3]),
        pltpu.make_async_copy(lc_h.at[0], lc, load.at[3]),
        pltpu.make_async_copy(order_h, order, load.at[4]),
    ]
    for copy in loads[:2]:
        copy.start()

    def at(x_, y_, z_, c_):
        return ((x_ % 4 * 8 + y_ % 8) * 2 + z_ % 2) * 2 + c_ % 2, sub

    pair0 = (mid, sub + 1 - 2 * v0)
    pair1 = (mid, sub + 2 - 4 * v1)
    pairz = at(x, y, zhi + 1, core)
    ypeer = [at(x, y + k, zhi, core) for k in range(8)]
    xpeer = [at(x + j // 2, y, zhi, core + j % 2) for j in range(8)]
    ysrc = [at(x, y + 8 - k, zhi, core) for k in range(8)]
    xsrc = [at(x + 4 - j // 2, y, zhi, core + j % 2) for j in range(8)]

    barrier = pltpu.get_barrier_semaphore()
    greet = [pair0, pair1, pairz] + ysrc[1:] + xsrc[1:]
    for peer in greet:
        pl.semaphore_signal(barrier, inc=1, device_id=peer, device_id_type=MESH)

    def half(v):
        return pl.ds(pl.multiple_of(v * 128, 128), 128)

    def swap(dst, src, rows, cols):
        for a, r in enumerate((rows, 1 - rows)):
            for b, q in enumerate((cols, 1 - cols)):
                dst[a * 128 : a * 128 + 128, b * 128 : b * 128 + 128] = src[half(r), half(q)]


    def remote(c, slot, src, dst, peer):
        pltpu.make_async_remote_copy(
            src_ref=src, dst_ref=dst, send_sem=send.at[0], recv_sem=recv.at[c, slot],
            device_id=peer, device_id_type=MESH,
        ).start()

    def arrived(c, slot, dst):
        pltpu.make_async_copy(dst, dst, recv.at[c, slot]).wait()

    def both(c, k):
        return jnp.concatenate([own[c][k], come[c][k]], axis=0)

    def split(c, k, slot, peer, matrix, value):
        outgo[c][k] = mm(matrix[128:256], value)
        remote(c, slot, outgo[c].at[k], come[c].at[k], peer)
        own[c][k] = mm(matrix[0:128], value)

    def stage(s, c):
        if s == 0:
            if c == 1:
                pltpu.make_async_copy(sig.at[1:N], sig.at[1:N], load.at[2]).wait()
            split(c, 0, RB0, pair0, cbt, sig[c])
        elif s == 1:
            arrived(c, RB0, come[c].at[0])
            split(c, 1, RB1, pair1, w0, both(c, 0))
        elif s == 2:
            arrived(c, RB1, come[c].at[1])
            value = both(c, 1)
            outgo[c][2] = mm(w1[128:256], value)
            remote(c, ZH, outgo[c].at[2], near[c].at[1], pairz)
            near[c][0] = mm(w1[0:128], value)
        elif s == 3:
            arrived(c, ZH, near[c].at[1])
            for k in (4, 3, 5, 2, 6, 1, 7):
                remote(c, YY, near[c].at[:, pl.ds(k * 16, 16)], ygot[c].at[k], ypeer[k])
        elif s == 4:
            arrived(c, YY, ygot[c].at[1:8])
            value = jnp.concatenate(
                [near[c][0, 0:16], near[c][1, 0:16]] + [ygot[c][k].reshape(32, WIDTHS[c]) for k in range(1, 8)],
                axis=0,
            )
            xsend[c][...] = mm(p2[...], value).reshape(8, 32, WIDTHS[c])
            for j in (4, 5, 2, 3, 6, 7, 1):
                remote(c, XC, xsend[c].at[j], xgot[c].at[j], xpeer[j])
        elif s == 5:
            arrived(c, XC, xgot[c].at[1:8])
            value = jnp.concatenate([xsend[c][0]] + [xgot[c][j] for j in range(1, 8)], axis=0)
            split(c, 3, LB1, pair1, w2, value)
        elif s == 6:
            arrived(c, LB1, come[c].at[3])
            split(c, 4, LB0, pair0, w3, both(c, 3))
        else:
            arrived(c, LB0, come[c].at[4])
            out[:, cols(c)] = mm(w4[...], both(c, 4))

    loads[0].wait()
    for copy in loads[2:]:
        copy.start()
    cbt[0:128] = cb[:, half(v0)].T
    cbt[128:256] = cb[:, half(1 - v0)].T

    def prepare():
        loads[-1].wait()
        r = iota((256, 128), 0)
        dest = (
            ((((r >> 2) & 3) + x & 3) * 8 + (((r >> 4) & 7) + y & 7)) * 4
            + ((r >> 7) + zhi & 1) * 2
            + (((r >> 1) & 1) + core & 1)
        )
        piece = jnp.sum(
            jnp.where(iota((256, 128), 1) == dest, order[...].astype(jnp.float32), 0.0),
            axis=1, keepdims=True,
        ).astype(jnp.int32)
        row, col = iota((256, 256), 0), iota((256, 256), 1)
        pick = onehot(col == piece * 2 + (row & 1))
        p2[...] = onehot(
            col == ((row >> 2) & 7) * 32 + ((row >> 1) & 1) * 16 + (row >> 5) * 2 + (row & 1)
        )
        sx, sc, sy, sz = col >> 6, (col >> 5) & 1, (col >> 2) & 7, (col >> 1) & 1
        source = (
            ((x + 4 - sx & 3) * 8 + (y + 8 - sy & 7)) * 4 + (zhi + sz & 1) * 2 + (core + sc & 1)
        ) * 2 + (col & 1)
        place = onehot(row == source)
        pltpu.make_async_copy(mats, mats, load.at[3]).wait()
        swap(w0, rc.at[0], v1, v0)
        for b, q in enumerate((v1, 1 - v1)):
            w3[:, b * 128 : b * 128 + 128] = rc[1, :, half(q)]
        w1[...] = mm(pick, w3[...])
        w4[...] = mm(mc[...], place)
        w2[0:128] = w4[half(v1), :]
        w2[128:256] = w4[half(1 - v1), :]
        swap(w3, lc.at[0], v0, v1)
        for b, q in enumerate((v0, 1 - v0)):
            w4[:, b * 128 : b * 128 + 128] = lc[1, :, half(q)]

    first = True
    for s, c in ORDER:
        if s == 0 and c == 0:
            loads[1].wait()
            pl.semaphore_wait(barrier, len(greet))
            split(0, 0, RB0, pair0, cbt, sig[0])
            continue
        if s == 1 and first:
            prepare()
            first = False
        stage(s, c)
    pltpu.make_async_copy(sent, sent, send.at[0]).wait()


def expand(rb, c5, out, tile, sem):
    rows = tile.shape[1]
    copies = []
    for i in range(tile.shape[0]):
        block = slice(i * rows, i * rows + rows)
        tile[i] = mm(rb[block], c5[...])
        copies.append(pltpu.make_async_copy(tile.at[i], out.at[block], sem.at[i]))
        copies[-1].start()
    for copy in copies:
        copy.wait()


def local(signal, col_basis, right_coupling, middle_coupling, left_coupling, row_basis, node_order):
    bf = jnp.bfloat16
    V = pltpu.VMEM
    hbm = pl.BlockSpec(memory_space=pl.ANY)
    vmem = pl.BlockSpec(memory_space=V)
    coeffs = pl.pallas_call(
        chain,
        name="chain",
        out_shape=V((256, signal.shape[1]), bf),
        in_specs=[hbm] * 6,
        out_specs=vmem,
        scratch_shapes=[
            V((1, 128), jnp.int32), V((N, 768, WIDTHS[0]), bf), V((768, 256), bf), V((5, 256, 256), bf), V((256, 768), bf),
        ]
        + [V((256, 256), bf)] * 6
        + [
            V((1088, signal.shape[1]), bf),
            pltpu.SemaphoreType.DMA((5,)),
            pltpu.SemaphoreType.DMA((1,)),
            pltpu.SemaphoreType.DMA((N, SLOTS)),
        ]
        + [
            V((*shape, width), bf)
            for shape in (
                (5, 128), (5, 128), (5, 128), (2, 128), (8, 2, 16), (8, 32), (8, 32)
            )
            for width in WIDTHS
        ],
        compiler_params=pltpu.CompilerParams(collective_id=0, has_side_effects=True, vmem_limit_bytes=CHAIN),
    )(signal, col_basis, right_coupling, middle_coupling, left_coupling, node_order.reshape(1, 128))
    rows, block = row_basis.shape[0], 128
    return pl.pallas_call(
        expand,
        name="expand",
        out_shape=jax.ShapeDtypeStruct((rows, signal.shape[1]), bf),
        in_specs=[vmem, vmem],
        out_specs=hbm,
        scratch_shapes=[
            V((rows // block, block, signal.shape[1]), bf), pltpu.SemaphoreType.DMA((rows // block,))
        ],
        compiler_params=pltpu.CompilerParams(vmem_limit_bytes=EXPAND),
    )(row_basis, coeffs)


def solution(mesh):
    return jax.shard_map(
        local,
        mesh=mesh,
        in_specs=(
            P(("mid", "sub"), None),
            P(("mid", "sub"), None),
            P(("mid", "sub"), None, None, None),
            P(("mid", "sub"), None, None),
            P(("mid", "sub"), None, None, None),
            P(("mid", "sub"), None),
            P(),
        ),
        out_specs=P(("mid", "sub"), None),
        check_vma=False,
    )
```

```python
import jax
import jax.numpy as jnp
from jax import lax
from jax.experimental import pallas as pl
from jax.experimental.pallas import tpu as pltpu
from jax.sharding import PartitionSpec as P

MESH = pl.DeviceIdType.MESH
CHAIN = 55 << 20
EXPAND = 8 << 20
WIDTHS = (128,) * 9
LAG = (0, 2, 5, 8, 11, 14, 17, 21)
N = len(WIDTHS)
START = [sum(WIDTHS[:c]) for c in range(N)]
ORDER = [(s, c) for _, _, s, c in sorted((c + LAG[s], -s, s, c) for s in range(8) for c in range(N))]
RB0, RB1, ZH, YY, XC, LB1, LB0, SLOTS = 0, 1, 2, 3, 4, 5, 6, 7


def iota(shape, dim):
    return lax.broadcasted_iota(jnp.int32, shape, dim)


def onehot(hit):
    return jnp.where(hit, 1.0, 0.0).astype(jnp.bfloat16)


def mm(a, b):
    return jnp.dot(a, b, preferred_element_type=jnp.float32).astype(jnp.bfloat16)


def chain(
    sig_h, cb_h, rc_h, mc_h, lc_h, order_h, out, order, sig, cb, mats, cbt, w0, w1, w2, w3, w4, p2,
    sent, load, send, recv, *bufs,
):
    mid, sub = lax.axis_index("mid"), lax.axis_index("sub")
    core, zhi, y, x = mid % 2, (mid // 2) % 2, (mid // 4) % 8, mid // 32
    v0, v1 = sub % 2, sub // 2

    def cols(c):
        return slice(START[c], START[c] + WIDTHS[c])

    own, outgo, come, near, ygot, xsend, xgot = (bufs[k * N : k * N + N] for k in range(7))
    rc, mc, lc = mats.at[0:2], mats.at[2], mats.at[3:5]

    loads = [pltpu.make_async_copy(cb_h, cb, load.at[0])]
    loads += [
        pltpu.make_async_copy(sig_h.at[:, cols(c)], sig.at[c], load.at[min(c, 1) + 1]) for c in range(N)
    ]
    loads += [
        pltpu.make_async_copy(rc_h.at[0], rc, load.at[3]),
        pltpu.make_async_copy(mc_h.at[0], mc, load.at[3]),
        pltpu.make_async_copy(lc_h.at[0], lc, load.at[3]),
        pltpu.make_async_copy(order_h, order, load.at[4]),
    ]
    for copy in loads[:2]:
        copy.start()

    def at(x_, y_, z_, c_):
        return ((x_ % 4 * 8 + y_ % 8) * 2 + z_ % 2) * 2 + c_ % 2, sub

    pair0 = (mid, sub + 1 - 2 * v0)
    pair1 = (mid, sub + 2 - 4 * v1)
    pairz = at(x, y, zhi + 1, core)
    ypeer = [at(x, y + k, zhi, core) for k in range(8)]
    xpeer = [at(x + j // 2, y, zhi, core + j % 2) for j in range(8)]
    ysrc = [at(x, y + 8 - k, zhi, core) for k in range(8)]
    xsrc = [at(x + 4 - j // 2, y, zhi, core + j % 2) for j in range(8)]

    barrier = pltpu.get_barrier_semaphore()
    greet = [pair0, pair1, pairz] + ysrc[1:] + xsrc[1:]
    for peer in greet:
        pl.semaphore_signal(barrier, inc=1, device_id=peer, device_id_type=MESH)

    def half(v):
        return pl.ds(pl.multiple_of(v * 128, 128), 128)

    def swap(dst, src, rows, cols):
        for a, r in enumerate((rows, 1 - rows)):
            for b, q in enumerate((cols, 1 - cols)):
                dst[a * 128 : a * 128 + 128, b * 128 : b * 128 + 128] = src[half(r), half(q)]


    def remote(c, slot, src, dst, peer):
        pltpu.make_async_remote_copy(
            src_ref=src, dst_ref=dst, send_sem=send.at[0], recv_sem=recv.at[c, slot],
            device_id=peer, device_id_type=MESH,
        ).start()

    def arrived(c, slot, dst):
        pltpu.make_async_copy(dst, dst, recv.at[c, slot]).wait()

    def both(c, k):
        return jnp.concatenate([own[c][k], come[c][k]], axis=0)

    def split(c, k, slot, peer, matrix, value):
        outgo[c][k] = mm(matrix[128:256], value)
        remote(c, slot, outgo[c].at[k], come[c].at[k], peer)
        own[c][k] = mm(matrix[0:128], value)

    def stage(s, c):
        if s == 0:
            if c == 1:
                pltpu.make_async_copy(sig.at[1:N], sig.at[1:N], load.at[2]).wait()
            split(c, 0, RB0, pair0, cbt, sig[c])
        elif s == 1:
            arrived(c, RB0, come[c].at[0])
            split(c, 1, RB1, pair1, w0, both(c, 0))
        elif s == 2:
            arrived(c, RB1, come[c].at[1])
            value = both(c, 1)
            outgo[c][2] = mm(w1[128:256], value)
            remote(c, ZH, outgo[c].at[2], near[c].at[1], pairz)
            near[c][0] = mm(w1[0:128], value)
        elif s == 3:
            arrived(c, ZH, near[c].at[1])
            for k in (4, 3, 5, 2, 6, 1, 7):
                remote(c, YY, near[c].at[:, pl.ds(k * 16, 16)], ygot[c].at[k], ypeer[k])
        elif s == 4:
            arrived(c, YY, ygot[c].at[1:8])
            value = jnp.concatenate(
                [near[c][0, 0:16], near[c][1, 0:16]] + [ygot[c][k].reshape(32, WIDTHS[c]) for k in range(1, 8)],
                axis=0,
            )
            xsend[c][...] = mm(p2[...], value).reshape(8, 32, WIDTHS[c])
            for j in (4, 5, 2, 3, 6, 7, 1):
                remote(c, XC, xsend[c].at[j], xgot[c].at[j], xpeer[j])
        elif s == 5:
            arrived(c, XC, xgot[c].at[1:8])
            value = jnp.concatenate([xsend[c][0]] + [xgot[c][j] for j in range(1, 8)], axis=0)
            split(c, 3, LB1, pair1, w2, value)
        elif s == 6:
            arrived(c, LB1, come[c].at[3])
            split(c, 4, LB0, pair0, w3, both(c, 3))
        else:
            arrived(c, LB0, come[c].at[4])
            out[:, cols(c)] = mm(w4[...], both(c, 4))

    loads[0].wait()
    for copy in loads[2:]:
        copy.start()
    cbt[0:128] = cb[:, half(v0)].T
    cbt[128:256] = cb[:, half(1 - v0)].T

    def prepare():
        loads[-1].wait()
        r = iota((256, 128), 0)
        dest = (
            ((((r >> 2) & 3) + x & 3) * 8 + (((r >> 4) & 7) + y & 7)) * 4
            + ((r >> 7) + zhi & 1) * 2
            + (((r >> 1) & 1) + core & 1)
        )
        piece = jnp.sum(
            jnp.where(iota((256, 128), 1) == dest, order[...].astype(jnp.float32), 0.0),
            axis=1, keepdims=True,
        ).astype(jnp.int32)
        row, col = iota((256, 256), 0), iota((256, 256), 1)
        pick = onehot(col == piece * 2 + (row & 1))
        p2[...] = onehot(
            col == ((row >> 2) & 7) * 32 + ((row >> 1) & 1) * 16 + (row >> 5) * 2 + (row & 1)
        )
        sx, sc, sy, sz = col >> 6, (col >> 5) & 1, (col >> 2) & 7, (col >> 1) & 1
        source = (
            ((x + 4 - sx & 3) * 8 + (y + 8 - sy & 7)) * 4 + (zhi + sz & 1) * 2 + (core + sc & 1)
        ) * 2 + (col & 1)
        place = onehot(row == source)
        pltpu.make_async_copy(mats, mats, load.at[3]).wait()
        swap(w0, rc.at[0], v1, v0)
        for b, q in enumerate((v1, 1 - v1)):
            w3[:, b * 128 : b * 128 + 128] = rc[1, :, half(q)]
        w1[...] = mm(pick, w3[...])
        w4[...] = mm(mc[...], place)
        w2[0:128] = w4[half(v1), :]
        w2[128:256] = w4[half(1 - v1), :]
        swap(w3, lc.at[0], v0, v1)
        for b, q in enumerate((v0, 1 - v0)):
            w4[:, b * 128 : b * 128 + 128] = lc[1, :, half(q)]

    first = True
    for s, c in ORDER:
        if s == 0 and c == 0:
            loads[1].wait()
            pl.semaphore_wait(barrier, len(greet))
            split(0, 0, RB0, pair0, cbt, sig[0])
            continue
        if s == 1 and first:
            prepare()
            first = False
        stage(s, c)
    pltpu.make_async_copy(sent, sent, send.at[0]).wait()


def expand(rb, c5, out, tile, sem):
    rows = tile.shape[1]
    copies = []
    for i in range(tile.shape[0]):
        block = slice(i * rows, i * rows + rows)
        tile[i] = mm(rb[block], c5[...])
        copies.append(pltpu.make_async_copy(tile.at[i], out.at[block], sem.at[i]))
        copies[-1].start()
    for copy in copies:
        copy.wait()


def local(signal, col_basis, right_coupling, middle_coupling, left_coupling, row_basis, node_order):
    bf = jnp.bfloat16
    V = pltpu.VMEM
    hbm = pl.BlockSpec(memory_space=pl.ANY)
    vmem = pl.BlockSpec(memory_space=V)
    coeffs = pl.pallas_call(
        chain,
        name="chain",
        out_shape=V((256, signal.shape[1]), bf),
        in_specs=[hbm] * 6,
        out_specs=vmem,
        scratch_shapes=[
            V((1, 128), jnp.int32), V((N, 768, WIDTHS[0]), bf), V((768, 256), bf), V((5, 256, 256), bf), V((256, 768), bf),
        ]
        + [V((256, 256), bf)] * 6
        + [
            V((1088, signal.shape[1]), bf),
            pltpu.SemaphoreType.DMA((5,)),
            pltpu.SemaphoreType.DMA((1,)),
            pltpu.SemaphoreType.DMA((N, SLOTS)),
        ]
        + [
            V((*shape, width), bf)
            for shape in (
                (5, 128), (5, 128), (5, 128), (2, 128), (8, 2, 16), (8, 32), (8, 32)
            )
            for width in WIDTHS
        ],
        compiler_params=pltpu.CompilerParams(collective_id=0, has_side_effects=True, vmem_limit_bytes=CHAIN),
    )(signal, col_basis, right_coupling, middle_coupling, left_coupling, node_order.reshape(1, 128))
    rows, block = row_basis.shape[0], 96
    return pl.pallas_call(
        expand,
        name="expand",
        out_shape=jax.ShapeDtypeStruct((rows, signal.shape[1]), bf),
        in_specs=[vmem, vmem],
        out_specs=hbm,
        scratch_shapes=[
            V((rows // block, block, signal.shape[1]), bf), pltpu.SemaphoreType.DMA((rows // block,))
        ],
        compiler_params=pltpu.CompilerParams(vmem_limit_bytes=EXPAND),
    )(row_basis, coeffs)


def solution(mesh):
    return jax.shard_map(
        local,
        mesh=mesh,
        in_specs=(
            P(("mid", "sub"), None),
            P(("mid", "sub"), None),
            P(("mid", "sub"), None, None, None),
            P(("mid", "sub"), None, None),
            P(("mid", "sub"), None, None, None),
            P(("mid", "sub"), None),
            P(),
        ),
        out_specs=P(("mid", "sub"), None),
        check_vma=False,
    )
```
